32 devices in a mesh: row: 4 (over y, x), col: 8 (over z, core).
Axes of the slice: x: 2, y: 2, z: 4, core: 2. Of those that a mesh axis runs over, the one named last changes fastest.
Arguments:
- boundary_start: float32 [16384, 128], P('row'), may hold values from -6 to 6
- volume_start: float32 [256, 512, 128], P(('row', 'col')), may hold values from -6 to 6
- diag_part: float32 [16384], P(('row', 'col')), may hold values from 1 to 2
- incident: float32 [16384, 128], P(('row', 'col')), may hold values from -6 to 6
- kernel: float32 [16384, 16384], P('row', 'col'), may hold values from -0.015625 to 0.015625
- elem_mats: float32 [256, 512, 512], P(('row', 'col')), may hold values from -0.078125 to 0.078125
- trace_owner: int32 [16384, 1], replicated, may hold values from 0 to 31; in each aligned block of 512 rows (0 to 511, 512 to 1023, ...) at most 32 rows name the same one
- trace_slot: int32 [16384], replicated, may hold values from 0 to 4095
- return_owner: int32 [16384, 1], replicated, may hold values from 0 to 31; in each aligned block of 512 rows (0 to 511, 512 to 1023, ...) at most 32 rows name the same one
- return_slot: int32 [16384], replicated, may hold values from 0 to 4095
- face_match: int32 [256, 64], P(('row', 'col')), may hold values from 0 to 63, each once within a row
Outputs:
- boundary_final: float32 [16384, 128], P('row')
- volume_final: float32 [256, 512, 128], P(('row', 'col'))
The draws below stay inside these ranges and needn't reach their ends.
Inputs may be any that keep to these rules, and one draw needn't show every extreme that they name: `trace_owner`: in each aligned block of 512 boundary rows (the rows of one device), no device is named more than 32 times; some device is named exactly 32 times in some block. `return_owner`: in each aligned block of 512 boundary rows (the rows of one device), no device is named more than 32 times; some device is named exactly 32 times in some block. `face_match`: each row is a permutation of 0 to 63.
All inputs are finite; a program needn't handle non-finite values.
Results may differ from the reference program's by a relative error of at most 0.0001.
Values sent between devices are 32-bit elements; how exact they have to be, the bound alone decides.
A program may use at most 128 MiB of HBM per device.

```python
import math
import jax
import jax.numpy as jnp
import numpy as np
from jax import lax

NB = 16384
R = 128
NODES = 512
FACE = 64
E_DEV = 8
ITERS = 3
ELEMS = 256
RB = 512
CAP = 32
DEVICES = 32


def set_ends(entries, own_key, smallest, top_value):
    index_at = [jax.random.randint(jax.random.fold_in(own_key, axis), (), 0, length) for axis, length in enumerate(entries.shape)]
    widest = entries.shape.index(max(entries.shape))
    beside = index_at[:widest] + [(index_at[widest] + 1) % entries.shape[widest]] + index_at[widest + 1:]
    return entries.at[tuple(index_at)].set(smallest).at[tuple(beside)].set(top_value)


def shard_levels(rng, dims, shards, low, high):
    factor_of, own = 1.0, jax.random.fold_in(rng, 6)
    for position, blocks in shards:
        heights = jnp.exp(jax.random.uniform(jax.random.fold_in(own, position), (blocks,), jnp.float32, low / len(shards), high / len(shards)))
        factor_of = factor_of * jnp.repeat(heights, dims[position] // blocks).reshape([-1 if axis == position else 1 for axis in range(len(dims))])
    return factor_of


def shared_out(key, own, number, rows, number_of, top, most, slope):
    sequence = jax.random.permutation(key, number_of)
    crowded, ordinary = shares(number_of, rows * top, most, slope, True), shares(number_of, rows * top, most, slope, False)
    places = jnp.arange(number_of)

    def named(tallies, turn):
        used = int((tallies > 0).sum())
        fixed = max(1, used // 4)
        shifted = fixed + (places - fixed + turn * (used - fixed)) % max(1, number_of - fixed)
        return jnp.zeros((number_of,), jnp.int32).at[sequence[jnp.where(places < fixed, places, shifted)]].set(jnp.asarray(tallies, jnp.int32))

    tallies = jnp.where(number % 4 == 0, named(crowded, number // 4), named(ordinary, number - number // 4 - 1))
    mixed = jax.random.permutation(jax.random.fold_in(own, 3), number_of)
    giver, sink = mixed[0:number_of // 2 * 2:2], mixed[1:number_of // 2 * 2:2]
    slack = jnp.minimum(tallies[giver] - 1, most - tallies[sink]) // 2
    slack = jnp.where((giver == sequence[0]) | (sink == sequence[0]) | (tallies[sink] == 0), 0, jnp.maximum(slack, 0))
    shifted = jax.random.randint(jax.random.fold_in(own, 4), (number_of // 2,), 0, 1 << 20) % (slack + 1)
    tallies = tallies.at[giver].add(-shifted).at[sink].add(shifted)
    members = jnp.searchsorted(jnp.cumsum(tallies), jnp.arange(rows * top), side="right").astype(jnp.int32)
    grid = members.reshape(top, rows).T
    grid = grid[jax.random.permutation(jax.random.fold_in(own, 1), rows)]
    turn = jax.random.randint(jax.random.fold_in(own, 2), (rows, 1), 0, top)
    return jnp.take_along_axis(grid, (jnp.arange(top)[None, :] + turn) % top, axis=1)


def shares(count, total, bound, lean, full):
    portions = [(1 << 20) // math.isqrt(rank ** lean) + 1 for rank in range(1, count + 1)]
    largest = bound if full else min(bound, max(-(-total // count), total * portions[0] // sum(portions)))
    least = 1 if total - largest >= count - 1 else 0
    given, spare = [largest] + [least] * (count - 1), total - largest - least * (count - 1)
    while spare > 0:
        candidates = [i for i in range(1, count) if given[i] < largest] or [i for i in range(1, count) if given[i] < bound]
        whole, left = sum([portions[i] for i in candidates]), spare
        for i in candidates:
            more = min(bound - given[i], max(1, left * portions[i] // whole), spare)
            given[i] = given[i] + more
            spare = spare - more
    return np.array(given)


def scatter_about(rng, dims, spread, bound, split=(), kind=jnp.bfloat16):
    values = spread * jax.random.normal(rng, dims, jnp.float32)
    if split:
        values = values * shard_levels(rng, dims, split, -0.22, 0.18)
    return jnp.clip(values, -bound, bound).astype(kind)


def setup_inputs(seed: int = 0) -> dict:
    splits = jax.random.split(jax.random.key(seed), 12)
    boundary_start = scatter_about(splits[0], (NB, R), 1.0, 6.0, ((0, 4),), jnp.float32)
    volume_start = scatter_about(splits[1], (ELEMS, NODES, R), 1.0, 6.0, ((0, 32),), jnp.float32)
    diag_part = jnp.clip(jnp.exp(math.log(2.0) - 0.6931472 * jax.random.uniform(splits[2], (NB,), jnp.float32) ** shard_levels(splits[2], (NB,), ((0, 32),), -0.2, 0.2)), 1.0, 2.0)
    incident = scatter_about(splits[3], (NB, R), 1.0, 6.0, ((0, 32),), jnp.float32)
    kernel = scatter_about(splits[4], (NB, NB), (8 * NB) ** -0.5, 0.015625, ((0, 4), (1, 8)), jnp.float32)
    elem_mats = scatter_about(splits[5], (ELEMS, NODES, NODES), (11 * NODES) ** -0.5, 0.078125, ((0, 32),), jnp.float32)
    trace_owner_keys = jax.random.split(jax.random.fold_in(splits[6], 1), NB // RB)
    trace_owner_turns = jax.random.permutation(jax.random.fold_in(splits[6], 3), NB // RB)
    trace_owner = jax.vmap(lambda own, number: shared_out(jax.random.fold_in(splits[6], 2), own, number, RB, DEVICES, 1, CAP, 1))(trace_owner_keys, trace_owner_turns).reshape((NB, 1))
    trace_slot = set_ends(jax.random.randint(splits[7], (NB,), 0, E_DEV * NODES), jax.random.fold_in(splits[7], 1), 0, (E_DEV * NODES) - 1).astype(jnp.int32)
    return_owner_keys = jax.random.split(jax.random.fold_in(splits[8], 1), NB // RB)
    return_owner_turns = jax.random.permutation(jax.random.fold_in(splits[8], 3), NB // RB)
    return_owner = jax.vmap(lambda own, number: shared_out(jax.random.fold_in(splits[8], 2), own, number, RB, DEVICES, 1, CAP, 2))(return_owner_keys, return_owner_turns).reshape((NB, 1))
    return_slot = set_ends(jax.random.randint(splits[9], (NB,), 0, E_DEV * NODES), jax.random.fold_in(splits[9], 1), 0, (E_DEV * NODES) - 1).astype(jnp.int32)
    face_match = jax.vmap(lambda own: jax.random.permutation(own, FACE))(jax.random.split(splits[10], ELEMS)).reshape((ELEMS, FACE)).astype(jnp.int32)
    return {"boundary_start": boundary_start, "volume_start": volume_start, "diag_part": diag_part, "incident": incident, "kernel": kernel, "elem_mats": elem_mats, "trace_owner": trace_owner, "trace_slot": trace_slot, "return_owner": return_owner, "return_slot": return_slot, "face_match": face_match}


boundary_step = 0.5
volume_step = 0.6
face_weight = 0.5


def reference(boundary_start, volume_start, diag_part, incident, kernel, elem_mats, trace_owner, trace_slot, return_owner, return_slot, face_match):
    highest = lax.Precision.HIGHEST
    owner_nodes = E_DEV * NODES
    trace_index = (trace_owner[:, 0] * owner_nodes + trace_slot).astype(jnp.int32)
    return_index = (return_owner[:, 0] * owner_nodes + return_slot).astype(jnp.int32)
    boundary = boundary_start
    volume = volume_start
    for sweep_index in range(ITERS):
        volume_flat = volume.reshape(ELEMS * NODES, R)
        traced = volume_flat[trace_index]
        image = jnp.dot(kernel, boundary, precision=highest, preferred_element_type=jnp.float32)
        residual = diag_part[:, None] * boundary + image - incident - traced
        flux_field = jnp.zeros_like(volume_flat).at[return_index].add(boundary).reshape(ELEMS, NODES, R)
        lower_faces = jnp.concatenate([jnp.zeros((E_DEV, FACE, R), jnp.float32), volume[:ELEMS - E_DEV, NODES - FACE:, :]], axis=0)
        matched = jax.vmap(lambda face_rows, face_order: face_rows[face_order])(lower_faces, face_match)
        applied = jnp.einsum("enm,emr->enr", elem_mats, volume, precision=highest)
        updated = volume - volume_step * (volume + applied - flux_field)
        volume = updated.at[:, :FACE, :].add(volume_step * face_weight * matched)
        boundary = boundary - boundary_step * residual
    return boundary, volume
```

```python
import jax
import jax.numpy as jnp
from jax import lax
from jax.sharding import PartitionSpec as P

ITERS = 3


boundary_step = 0.5
volume_step = 0.6
face_weight = 0.5


def passed_along(block, axis, distance):
    devices = range(lax.axis_size(axis))
    route = [(i - distance, i) for i in devices if i - distance in devices]
    return lax.ppermute(block, axis, route)


def halves(block, axis):
    high = lax.reduce_precision(block, 8, 7)
    low = block - high
    return jnp.concatenate([high.astype(jnp.bfloat16), low.astype(jnp.bfloat16)], axis=axis)


def summed(wide, columns):
    return wide[..., :columns] + wide[..., columns:]


def block_plan(owner_blocks, slot_blocks, device_self, capacity):
    mine_rows = owner_blocks == device_self
    rank_rows = jnp.cumsum(mine_rows.astype(jnp.int32), axis=1) - 1
    places = jnp.arange(capacity, dtype=jnp.int32)
    select = mine_rows[:, None, :] & (rank_rows[:, None, :] == places[None, :, None])
    index = jnp.sum(jnp.where(select, slot_blocks[:, None, :], 0), axis=2)
    valid_slot = jnp.any(select, axis=2)
    return (index, valid_slot)


def shards(
    boundary_start,
    volume_start,
    diag_part,
    incident,
    kernel,
    elem_mats,
    trace_owner,
    trace_slot,
    return_owner,
    return_slot,
    face_match,
):
    devices = lax.axis_size(("row", "col"))
    row_devices = lax.axis_size("row")
    col_devices = lax.axis_size("col")
    device_self = lax.axis_index(("row", "col"))
    row_index = lax.axis_index("row")
    col_index = lax.axis_index("col")
    total_rows = trace_slot.shape[0]
    share_rows = total_rows // devices
    capacity = max(2, 2 * share_rows // devices)
    per_panel = col_devices // row_devices
    elem_count, node_count, columns = volume_start.shape
    face_count = face_match.shape[1]
    row_panel = boundary_start.shape[0]
    positions = jnp.arange(share_rows, dtype=jnp.int32)
    trace_blocks = trace_owner[:, 0].reshape(devices, share_rows)
    trace_slots = trace_slot.reshape(devices, share_rows)
    return_blocks = return_owner[:, 0].reshape(devices, share_rows)
    return_slots = return_slot.reshape(devices, share_rows)

    route = []
    for c in range(col_devices):
        for j in range(row_devices):
            source = (c // per_panel) * col_devices + (c % per_panel) * row_devices + j
            route.append((source, j * col_devices + c))

    trace_send, trace_send_ok = block_plan(trace_blocks, trace_slots, device_self, capacity)
    own_trace = lax.dynamic_slice_in_dim(trace_blocks, row_index * col_devices, col_devices, 0)
    block_places = jnp.arange(col_devices, dtype=jnp.int32)[:, None] * share_rows + positions[None, :]
    trace_take = jax.vmap(lambda r: block_plan(own_trace, block_places, r * col_devices + col_index, capacity)[0])(
        jnp.arange(row_devices, dtype=jnp.int32)
    )
    own_return = lax.dynamic_slice_in_dim(return_blocks, col_index * row_devices, row_devices, 0)
    panel_places = jnp.arange(row_devices, dtype=jnp.int32)[:, None] * share_rows + positions[None, :]
    flux_send, flux_send_ok = jax.vmap(
        lambda d: block_plan(own_return, panel_places, row_index * col_devices + d, capacity)
    )(jnp.arange(col_devices, dtype=jnp.int32))
    flux_take, _ = block_plan(return_blocks, return_slots, device_self, capacity)
    slots = devices * capacity
    trace_send, trace_send_ok = trace_send.reshape(slots), trace_send_ok.reshape(slots, 1)
    flux_send, flux_send_ok = flux_send.reshape(slots), flux_send_ok.reshape(slots, 1)
    trace_take, flux_take = trace_take.reshape(slots), flux_take.reshape(slots)

    kernel_halves = halves(kernel, 1)
    elem_halves = halves(elem_mats, 2)
    share = lax.dynamic_slice_in_dim(boundary_start, col_index * share_rows, share_rows, 0)
    volume_field = volume_start
    for sweep_index in range(ITERS):
        moved = lax.ppermute(share, ("row", "col"), route)
        panel = lax.all_gather(moved, "row", axis=0, tiled=True)

        volume_flat = volume_field.reshape(elem_count * node_count, columns)
        outgoing = jnp.where(trace_send_ok, volume_flat[trace_send], 0.0)
        arrived = lax.all_to_all(outgoing, "row", split_axis=0, concat_axis=0, tiled=True)
        traced = jnp.zeros((row_panel, columns), jnp.float32).at[trace_take].add(arrived)

        wide = halves(panel, 1)
        image = summed(
            jnp.dot(kernel_halves, jnp.concatenate([wide, wide], 0), preferred_element_type=jnp.float32),
            columns,
        )
        residual = lax.psum_scatter(image - traced, "col", scatter_dimension=0, tiled=True)
        share = share - boundary_step * (residual + (diag_part[:, None] * share - incident))

        leaving = jnp.where(flux_send_ok, panel[flux_send], 0.0)
        landed = lax.all_to_all(leaving, "col", split_axis=0, concat_axis=0, tiled=True)
        flux_field = jnp.zeros_like(volume_flat).at[flux_take].add(landed).reshape(volume_field.shape)
        lower_faces = passed_along(volume_field[:, node_count - face_count :, :], ("row", "col"), 1)
        matched = jax.vmap(lambda face_rows, face_order: face_rows[face_order])(lower_faces, face_match)
        volume_wide = halves(volume_field, 2)
        applied = summed(
            jnp.einsum(
                "enm,emr->enr",
                elem_halves,
                jnp.concatenate([volume_wide, volume_wide], 1),
                preferred_element_type=jnp.float32,
            ),
            columns,
        )
        updated = volume_field - volume_step * (volume_field + applied - flux_field)
        volume_field = updated.at[:, :face_count, :].add(volume_step * face_weight * matched)
    boundary_final = lax.all_gather(share, "col", axis=0, tiled=True)
    return (boundary_final, volume_field)


def solution(mesh):
    placed = (
        P("row", None),
        P(("row", "col"), None, None),
        P(("row", "col")),
        P(("row", "col"), None),
        P("row", "col"),
        P(("row", "col"), None, None),
        P(),
        P(),
        P(),
        P(),
        P(("row", "col"), None),
    )
    return jax.shard_map(
        shards,
        mesh=mesh,
        in_specs=placed,
        out_specs=(P("row", None), P(("row", "col"), None, None)),
        check_vma=False,
    )
```

```python
import functools

import jax
import jax.numpy as jnp
from jax import lax
from jax.experimental import pallas as pl
from jax.experimental.pallas import tpu as pltpu
from jax.sharding import PartitionSpec as P

ITERS = 3


boundary_step = 0.5
volume_step = 0.6
face_weight = 0.5


def passed_along(block, axis, distance):
    devices = range(lax.axis_size(axis))
    route = [(i - distance, i) for i in devices if i - distance in devices]
    return lax.ppermute(block, axis, route)


def exchange_kernel(reduces, finishes, *refs):
    rows_n, cols_n = lax.axis_size("row"), lax.axis_size("col")
    pairs = cols_n // 2
    per_panel = cols_n // rows_n
    r, c = lax.axis_index("row"), lax.axis_index("col")
    z, h = c // 2, c % 2
    partner = z * 2 + (1 - h)
    target_row, target_col = c % rows_n, r * per_panel + c // rows_n
    source_row, source_col = c // per_panel, (c % per_panel) * rows_n + r
    stays = (target_row == r) & (target_col == c)

    if reduces:
        partial, middle, refs = refs[0], refs[1], refs[2:]
    else:
        middle, refs = refs[0], refs[1:]
    if finishes:
        out, refs = refs[0], refs[1:]
    else:
        share, out, refs = refs[0], refs[1], refs[2:]
    if reduces:
        from_pair, summed_pair, from_line, refs = refs[0], refs[1], refs[2], refs[3:]
        pair_send, pair_recv, line_send, line_recv, refs = refs[0], refs[1], refs[2], refs[3], refs[4:]
    if finishes:
        out_send, out_recv, back_send, back_recv = refs
    else:
        move_send, move_recv, row_send, row_recv = refs

    barrier = pltpu.get_barrier_semaphore()

    def greet(row, col):
        pl.semaphore_signal(barrier, inc=1, device_id=(row, col), device_id_type=pl.DeviceIdType.MESH)

    greeted = 0
    if reduces:
        greet(r, partner)
        for step in range(1, pairs):
            greet(r, ((z + step) % pairs) * 2 + h)
        greeted += pairs
    if not finishes:
        for step in range(1, rows_n):
            greet((r + step) % rows_n, c)
        greeted += rows_n - 1

        @pl.when(jnp.logical_not(stays))
        def _():
            greet(source_row, source_col)

        greeted += jnp.where(stays, 0, 1)

    pl.semaphore_wait(barrier, greeted)

    def remote(src, dst, send, recv, row, col):
        return pltpu.make_async_remote_copy(
            src_ref=src,
            dst_ref=dst,
            send_sem=send,
            recv_sem=recv,
            device_id=(row, col),
            device_id_type=pl.DeviceIdType.MESH,
        )

    if reduces:
        pair_copies = []
        for step in range(1, pairs + 1):
            other = (z + step) % pairs
            copy = remote(
                partial.at[other * 2 + (1 - h)], from_pair.at[step - 1],
                pair_send.at[step - 1], pair_recv.at[step - 1], r, partner,
            )
            copy.start()
            pair_copies.append(copy)
        line_copies = []
        for step in range(1, pairs):
            other = (z + step) % pairs
            pair_copies[step - 1].wait_recv()
            summed_pair[step - 1] = from_pair[step - 1] + partial[other * 2 + h]
            copy = remote(
                summed_pair.at[step - 1], from_line.at[step - 1],
                line_send.at[step - 1], line_recv.at[step - 1], r, other * 2 + h,
            )
            copy.start()
            line_copies.append(copy)
        pair_copies[pairs - 1].wait_recv()
        total = from_pair[pairs - 1] + partial[z * 2 + h]
        summed_pair[pairs - 1] = total
        for step in range(1, pairs):
            line_copies[step - 1].wait_recv()
            summed_pair[pairs - 1] += from_line[step - 1]
        fresh = middle[...] - boundary_step * summed_pair[pairs - 1]
        if finishes:
            out[c] = fresh
        else:
            share[...] = fresh
    else:
        share[...] = middle[...]

    if finishes:
        sent = []
        for step in range(1, pairs):
            copy = remote(
                out.at[c], out.at[c], out_send.at[step - 1], out_recv.at[step - 1],
                r, ((z + step) % pairs) * 2 + h,
            )
            copy.start()
            sent.append(copy)
        back = [remote(out.at[c], out.at[c], back_send.at[0], back_recv.at[0], r, partner)]
        back[0].start()
        for step in range(1, pairs):
            origin = ((z - step + pairs) % pairs) * 2 + h
            sent[step - 1].wait_recv()
            copy = remote(
                out.at[origin], out.at[origin], back_send.at[step], back_recv.at[step], r, partner
            )
            copy.start()
            back.append(copy)
        for copy in back:
            copy.wait_recv()
        for copy in sent + back:
            copy.wait_send()
    else:
        @pl.when(stays)
        def _():
            out[r] = share[...]

        move = remote(share, out.at[target_row], move_send, move_recv, target_row, target_col)

        @pl.when(jnp.logical_not(stays))
        def _():
            move.start()
            move.wait_recv()

        sent = []
        for step in range(1, rows_n):
            copy = remote(
                out.at[r], out.at[r], row_send.at[step - 1], row_recv.at[step - 1],
                (r + step) % rows_n, c,
            )
            copy.start()
            sent.append(copy)
        for copy in sent:
            copy.wait_recv()
        for copy in sent:
            copy.wait_send()

        @pl.when(jnp.logical_not(stays))
        def _():
            move.wait_send()

    if reduces:
        for copy in pair_copies + line_copies:
            copy.wait_send()


def exchange(reduces, finishes, *operands):
    rows_n, cols_n = lax.axis_size("row"), lax.axis_size("col")
    pairs = cols_n // 2
    rows, columns = operands[-1].shape
    block = (rows, columns)
    in_vmem = pl.BlockSpec(memory_space=pltpu.VMEM)
    if finishes:
        shapes = [jax.ShapeDtypeStruct((cols_n,) + block, jnp.float32)]
    else:
        shapes = [
            jax.ShapeDtypeStruct(block, jnp.float32),
            jax.ShapeDtypeStruct((rows_n,) + block, jnp.float32),
        ]
    scratch = []
    if reduces:
        scratch += [pltpu.VMEM((pairs,) + block, jnp.float32), pltpu.VMEM((pairs,) + block, jnp.float32)]
        scratch += [pltpu.VMEM((pairs - 1,) + block, jnp.float32)]
        scratch += [pltpu.SemaphoreType.DMA((pairs,))] * 2 + [pltpu.SemaphoreType.DMA((pairs - 1,))] * 2
    if finishes:
        scratch += [pltpu.SemaphoreType.DMA((pairs - 1,))] * 2 + [pltpu.SemaphoreType.DMA((pairs,))] * 2
    else:
        scratch += [pltpu.SemaphoreType.DMA] * 2 + [pltpu.SemaphoreType.DMA((rows_n - 1,))] * 2
    return pl.pallas_call(
        functools.partial(exchange_kernel, reduces, finishes),
        out_shape=shapes,
        in_specs=[in_vmem] * len(operands),
        out_specs=[in_vmem] * len(shapes),
        scratch_shapes=scratch,
        compiler_params=pltpu.CompilerParams(
            collective_id=int(reduces) + int(finishes), has_side_effects=True, vmem_limit_bytes=24 << 20
        ),
        cost_estimate=pl.CostEstimate(flops=1000, bytes_accessed=150_000_000, transcendentals=0),
    )(*operands)


def halves(block, axis):
    high = lax.reduce_precision(block, 8, 7)
    low = block - high
    return jnp.concatenate([high.astype(jnp.bfloat16), low.astype(jnp.bfloat16)], axis=axis)


def summed(wide, columns):
    return wide[..., :columns] + wide[..., columns:]


def block_plan(owner_blocks, slot_blocks, device_self, capacity):
    mine_rows = owner_blocks == device_self
    rank_rows = jnp.cumsum(mine_rows.astype(jnp.int32), axis=1) - 1
    places = jnp.arange(capacity, dtype=jnp.int32)
    select = mine_rows[:, None, :] & (rank_rows[:, None, :] == places[None, :, None])
    index = jnp.sum(jnp.where(select, slot_blocks[:, None, :], 0), axis=2)
    valid_slot = jnp.any(select, axis=2)
    return (index, valid_slot)


def shards(
    boundary_start,
    volume_start,
    diag_part,
    incident,
    kernel,
    elem_mats,
    trace_owner,
    trace_slot,
    return_owner,
    return_slot,
    face_match,
):
    devices = lax.axis_size(("row", "col"))
    row_devices = lax.axis_size("row")
    col_devices = lax.axis_size("col")
    device_self = lax.axis_index(("row", "col"))
    row_index = lax.axis_index("row")
    col_index = lax.axis_index("col")
    total_rows = trace_slot.shape[0]
    share_rows = total_rows // devices
    capacity = max(2, 2 * share_rows // devices)
    per_panel = col_devices // row_devices
    elem_count, node_count, columns = volume_start.shape
    face_count = face_match.shape[1]
    row_panel = boundary_start.shape[0]
    positions = jnp.arange(share_rows, dtype=jnp.int32)
    trace_blocks = trace_owner[:, 0].reshape(devices, share_rows)
    trace_slots = trace_slot.reshape(devices, share_rows)
    return_blocks = return_owner[:, 0].reshape(devices, share_rows)
    return_slots = return_slot.reshape(devices, share_rows)

    trace_send, trace_send_ok = block_plan(trace_blocks, trace_slots, device_self, capacity)
    own_trace = lax.dynamic_slice_in_dim(trace_blocks, row_index * col_devices, col_devices, 0)
    block_places = jnp.arange(col_devices, dtype=jnp.int32)[:, None] * share_rows + positions[None, :]
    trace_take = jax.vmap(lambda r: block_plan(own_trace, block_places, r * col_devices + col_index, capacity)[0])(
        jnp.arange(row_devices, dtype=jnp.int32)
    )
    own_return = lax.dynamic_slice_in_dim(return_blocks, col_index * row_devices, row_devices, 0)
    panel_places = jnp.arange(row_devices, dtype=jnp.int32)[:, None] * share_rows + positions[None, :]
    flux_send, flux_send_ok = jax.vmap(
        lambda d: block_plan(own_return, panel_places, row_index * col_devices + d, capacity)
    )(jnp.arange(col_devices, dtype=jnp.int32))
    flux_take, _ = block_plan(return_blocks, return_slots, device_self, capacity)
    slots = devices * capacity
    trace_send, trace_send_ok = trace_send.reshape(slots), trace_send_ok.reshape(slots, 1)
    flux_send, flux_send_ok = flux_send.reshape(slots), flux_send_ok.reshape(slots, 1)
    trace_take, flux_take = trace_take.reshape(slots), flux_take.reshape(slots)

    kernel_halves = halves(kernel, 1)
    elem_halves = halves(elem_mats, 2)
    share = lax.dynamic_slice_in_dim(boundary_start, col_index * share_rows, share_rows, 0)
    share, panel = exchange(False, False, share)
    volume_field = volume_start
    for sweep_index in range(ITERS):
        panel = panel.reshape(row_devices * share_rows, columns)

        volume_flat = volume_field.reshape(elem_count * node_count, columns)
        outgoing = jnp.where(trace_send_ok, volume_flat[trace_send], 0.0)
        arrived = lax.all_to_all(outgoing, "row", split_axis=0, concat_axis=0, tiled=True)
        traced = jnp.zeros((row_panel, columns), jnp.float32).at[trace_take].add(arrived)

        wide = halves(panel, 1)
        image = summed(
            jnp.dot(kernel_halves, jnp.concatenate([wide, wide], 0), preferred_element_type=jnp.float32),
            columns,
        )
        partial_value = (image - traced).reshape(col_devices, share_rows, columns)
        middle = share - boundary_step * (diag_part[:, None] * share - incident)
        leaving = jnp.where(flux_send_ok, panel[flux_send], 0.0)
        landed = lax.all_to_all(leaving, "col", split_axis=0, concat_axis=0, tiled=True)
        flux_field = jnp.zeros_like(volume_flat).at[flux_take].add(landed).reshape(volume_field.shape)
        lower_faces = passed_along(volume_field[:, node_count - face_count :, :], ("row", "col"), 1)
        matched = jax.vmap(lambda face_rows, face_order: face_rows[face_order])(lower_faces, face_match)
        volume_wide = halves(volume_field, 2)
        applied = summed(
            jnp.einsum(
                "enm,emr->enr",
                elem_halves,
                jnp.concatenate([volume_wide, volume_wide], 1),
                preferred_element_type=jnp.float32,
            ),
            columns,
        )
        updated = volume_field - volume_step * (volume_field + applied - flux_field)
        volume_field = updated.at[:, :face_count, :].add(volume_step * face_weight * matched)
        if sweep_index < ITERS - 1:
            share, panel = exchange(True, False, partial_value, middle)
        else:
            (boundary_final,) = exchange(True, True, partial_value, middle)
    return (boundary_final.reshape(row_panel, columns), volume_field)


def solution(mesh):
    placed = (
        P("row", None),
        P(("row", "col"), None, None),
        P(("row", "col")),
        P(("row", "col"), None),
        P("row", "col"),
        P(("row", "col"), None, None),
        P(),
        P(),
        P(),
        P(),
        P(("row", "col"), None),
    )
    return jax.shard_map(
        shards,
        mesh=mesh,
        in_specs=placed,
        out_specs=(P("row", None), P(("row", "col"), None, None)),
        check_vma=False,
    )
```

```python
import functools

import jax
import jax.numpy as jnp
from jax import lax
from jax.experimental import pallas as pl
from jax.experimental.pallas import tpu as pltpu
from jax.sharding import PartitionSpec as P

ITERS = 3


boundary_step = 0.5
volume_step = 0.6
face_weight = 0.5


def passed_along(block, axis, distance):
    devices = range(lax.axis_size(axis))
    route = [(i - distance, i) for i in devices if i - distance in devices]
    return lax.ppermute(block, axis, route)


def exchange_kernel(reduces, finishes, *refs):
    rows_n, cols_n = lax.axis_size("row"), lax.axis_size("col")
    pairs = cols_n // 2
    per_panel = cols_n // rows_n
    r, c = lax.axis_index("row"), lax.axis_index("col")
    z, h = c // 2, c % 2
    partner = z * 2 + (1 - h)
    target_row, target_col = c % rows_n, r * per_panel + c // rows_n
    source_row, source_col = c // per_panel, (c % per_panel) * rows_n + r
    stays = (target_row == r) & (target_col == c)

    if reduces:
        panel_wide, trace_wide, trace_take, kernel, elem_mats, volume = refs[:6]
        flux_wide, flux_take, face_wide, face_match, middle, volume_out = refs[6:12]
        refs = refs[12:]
    else:
        middle, refs = refs[0], refs[1:]
    if finishes:
        out, refs = refs[0], refs[1:]
    else:
        share, out, refs = refs[0], refs[1], refs[2:]
    if reduces:
        from_pair, summed_pair, from_line, refs = refs[0], refs[1], refs[2], refs[3:]
        pair_send, pair_recv, line_send, line_recv, refs = refs[0], refs[1], refs[2], refs[3], refs[4:]
        partial, kernel_blocks, elem_blocks, kernel_sem, elem_sem = refs[:5]
        refs = refs[5:]
    if finishes:
        out_send, out_recv, back_send, back_recv = refs
    else:
        move_send, move_recv, row_send, row_recv = refs

    barrier = pltpu.get_barrier_semaphore()

    def greet(row, col):
        pl.semaphore_signal(barrier, inc=1, device_id=(row, col), device_id_type=pl.DeviceIdType.MESH)

    greeted = 0
    if reduces:
        greet(r, partner)
        for step in range(1, pairs):
            greet(r, ((z + step) % pairs) * 2 + h)
        greeted += pairs
    if not finishes:
        for step in range(1, rows_n):
            greet((r + step) % rows_n, c)
        greeted += rows_n - 1

        @pl.when(jnp.logical_not(stays))
        def _():
            greet(source_row, source_col)

        greeted += jnp.where(stays, 0, 1)

    pl.semaphore_wait(barrier, greeted)

    def remote(src, dst, send, recv, row, col):
        return pltpu.make_async_remote_copy(
            src_ref=src,
            dst_ref=dst,
            send_sem=send,
            recv_sem=recv,
            device_id=(row, col),
            device_id_type=pl.DeviceIdType.MESH,
        )

    if reduces:
        share_rows, columns = middle.shape
        tile = min(128, share_rows)
        elem_count, node_count, _ = volume.shape
        face_count = face_match.shape[1]

        def parts(block):
            high = block.astype(jnp.bfloat16)
            low = (block - high.astype(jnp.float32)).astype(jnp.bfloat16)
            return high, low

        def product(left, right):
            return jnp.dot(left, right, preferred_element_type=jnp.float32)

        def one_hot(hits):
            return jnp.where(hits, 1.0, 0.0).astype(jnp.bfloat16)

        def product_block(block, slot):
            def step(t, carry):
                rows = pl.ds(pl.multiple_of(t * tile, tile), tile)
                high, low = parts(kernel_blocks[slot, rows, :])
                place = lax.broadcasted_iota(jnp.int32, (tile, trace_wide.shape[1]), 0) + t * tile
                wide = product(high, panel_wide[...]) + product(low, panel_wide[...])
                wide -= product(one_hot(place == trace_take[block]), trace_wide[block])
                partial[block, rows, :] = wide[:, :columns] + wide[:, columns:]
                return carry

            lax.fori_loop(0, share_rows // tile, step, 0)

        def volume_step_of(e, carry):
            field = volume[e]
            high, low = parts(elem_blocks[e])
            field_wide = jnp.concatenate(parts(field), axis=1)
            wide = product(high, field_wide) + product(low, field_wide)
            place = lax.broadcasted_iota(jnp.int32, (node_count, flux_wide.shape[0]), 0) + e * node_count
            wide -= product(one_hot(place == flux_take[...]), flux_wide[...])
            volume_out[e] = field - volume_step * (field + wide[:, :columns] + wide[:, columns:])
            node = lax.broadcasted_iota(jnp.int32, (face_count, face_count), 1)
            face = product(one_hot(node == face_match[e]), face_wide[e])
            matched = face[:, :columns] + face[:, columns:]
            volume_out[e, :face_count, :] += volume_step * face_weight * matched
            return carry

        elem_load = pltpu.make_async_copy(elem_mats, elem_blocks, elem_sem)
        order = []
        for step in range(1, pairs + 1):
            other = (z + step) % pairs
            order += [other * 2 + (1 - h), other * 2 + h]

        def load(i):
            return pltpu.make_async_copy(
                kernel.at[pl.ds(pl.multiple_of(order[i] * share_rows, share_rows), share_rows), :],
                kernel_blocks.at[i % 2],
                kernel_sem.at[i % 2],
            )

        load(0).start()
        pair_copies = []
        line_copies = []

        def pass_on(step):
            other = (z + step) % pairs
            pair_copies[step - 1].wait_recv()
            summed_pair[step - 1] = from_pair[step - 1] + partial[other * 2 + h]
            copy = remote(
                summed_pair.at[step - 1], from_line.at[step - 1],
                line_send.at[step - 1], line_recv.at[step - 1], r, other * 2 + h,
            )
            copy.start()
            line_copies.append(copy)

        for i in range(2 * pairs):
            if i + 1 < 2 * pairs:
                load(i + 1).start()
            load(i).wait()
            product_block(order[i], i % 2)
            if i % 2 == 0:
                copy = remote(
                    partial.at[order[i]], from_pair.at[i // 2],
                    pair_send.at[i // 2], pair_recv.at[i // 2], r, partner,
                )
                copy.start()
                pair_copies.append(copy)
            elif i // 2 + 1 < pairs:
                pass_on(i // 2 + 1)
        elem_load.start()
        elem_load.wait()
        lax.fori_loop(0, elem_count // 2, volume_step_of, 0)
        pair_copies[pairs - 1].wait_recv()
        total = from_pair[pairs - 1] + partial[z * 2 + h]
        summed_pair[pairs - 1] = total
        for step in range(1, pairs):
            line_copies[step - 1].wait_recv()
            summed_pair[pairs - 1] += from_line[step - 1]
        fresh = middle[...] - boundary_step * summed_pair[pairs - 1]
        if finishes:
            out[c] = fresh
        else:
            share[...] = fresh
    else:
        share[...] = middle[...]

    if finishes:
        sent = []
        for step in range(1, pairs):
            copy = remote(
                out.at[c], out.at[c], out_send.at[step - 1], out_recv.at[step - 1],
                r, ((z + step) % pairs) * 2 + h,
            )
            copy.start()
            sent.append(copy)
        back = [remote(out.at[c], out.at[c], back_send.at[0], back_recv.at[0], r, partner)]
        back[0].start()
        for step in range(1, pairs):
            origin = ((z - step + pairs) % pairs) * 2 + h
            sent[step - 1].wait_recv()
            copy = remote(
                out.at[origin], out.at[origin], back_send.at[step], back_recv.at[step], r, partner
            )
            copy.start()
            back.append(copy)
        if reduces:
            lax.fori_loop(elem_count // 2, elem_count, volume_step_of, 0)
        for copy in back:
            copy.wait_recv()
        for copy in sent + back:
            copy.wait_send()
    else:
        @pl.when(stays)
        def _():
            out[r] = share[...]

        move = remote(share, out.at[target_row], move_send, move_recv, target_row, target_col)

        @pl.when(jnp.logical_not(stays))
        def _():
            move.start()
            move.wait_recv()

        sent = []
        for step in range(1, rows_n):
            copy = remote(
                out.at[r], out.at[r], row_send.at[step - 1], row_recv.at[step - 1],
                (r + step) % rows_n, c,
            )
            copy.start()
            sent.append(copy)
        if reduces:
            lax.fori_loop(elem_count // 2, elem_count, volume_step_of, 0)
        for copy in sent:
            copy.wait_recv()
        for copy in sent:
            copy.wait_send()

        @pl.when(jnp.logical_not(stays))
        def _():
            move.wait_send()

    if reduces:
        for copy in pair_copies + line_copies:
            copy.wait_send()


def exchange(reduces, finishes, *operands):
    rows_n, cols_n = lax.axis_size("row"), lax.axis_size("col")
    pairs = cols_n // 2
    rows, columns = operands[-1].shape
    block = (rows, columns)
    in_vmem = pl.BlockSpec(memory_space=pltpu.VMEM)
    if finishes:
        shapes = [jax.ShapeDtypeStruct((cols_n,) + block, jnp.float32)]
    else:
        shapes = [
            jax.ShapeDtypeStruct(block, jnp.float32),
            jax.ShapeDtypeStruct((rows_n,) + block, jnp.float32),
        ]
    scratch = []
    in_specs = [in_vmem] * len(operands)
    if reduces:
        kernel, elem_mats, volume = operands[3:6]
        shapes = [jax.ShapeDtypeStruct(volume.shape, jnp.float32)] + shapes
        in_specs[3] = in_specs[4] = pl.BlockSpec(memory_space=pl.ANY)
        scratch += [pltpu.VMEM((pairs,) + block, jnp.float32), pltpu.VMEM((pairs,) + block, jnp.float32)]
        scratch += [pltpu.VMEM((pairs - 1,) + block, jnp.float32)]
        scratch += [pltpu.SemaphoreType.DMA((pairs,))] * 2 + [pltpu.SemaphoreType.DMA((pairs - 1,))] * 2
        scratch += [
            pltpu.VMEM((cols_n,) + block, jnp.float32),
            pltpu.VMEM((2, rows, kernel.shape[1]), jnp.float32),
            pltpu.VMEM(elem_mats.shape, jnp.float32),
            pltpu.SemaphoreType.DMA((2,)),
            pltpu.SemaphoreType.DMA,
        ]
    if finishes:
        scratch += [pltpu.SemaphoreType.DMA((pairs - 1,))] * 2 + [pltpu.SemaphoreType.DMA((pairs,))] * 2
    else:
        scratch += [pltpu.SemaphoreType.DMA] * 2 + [pltpu.SemaphoreType.DMA((rows_n - 1,))] * 2
    return pl.pallas_call(
        functools.partial(exchange_kernel, reduces, finishes),
        out_shape=shapes,
        in_specs=in_specs,
        out_specs=[in_vmem] * len(shapes),
        scratch_shapes=scratch,
        compiler_params=pltpu.CompilerParams(
            collective_id=int(reduces) + int(finishes), has_side_effects=True, vmem_limit_bytes=(48 << 20) if reduces else (8 << 20)
        ),
        cost_estimate=pl.CostEstimate(flops=1000, bytes_accessed=150_000_000, transcendentals=0),
    )(*operands)


def halves(block, axis):
    high = lax.reduce_precision(block, 8, 7)
    low = block - high
    return jnp.concatenate([high.astype(jnp.bfloat16), low.astype(jnp.bfloat16)], axis=axis)


def block_plan(owner_blocks, slot_blocks, device_self, capacity):
    mine_rows = owner_blocks == device_self
    rank_rows = jnp.cumsum(mine_rows.astype(jnp.int32), axis=1) - 1
    places = jnp.arange(capacity, dtype=jnp.int32)
    select = mine_rows[:, None, :] & (rank_rows[:, None, :] == places[None, :, None])
    index = jnp.sum(jnp.where(select, slot_blocks[:, None, :], 0), axis=2)
    valid_slot = jnp.any(select, axis=2)
    return (index, valid_slot)


def shards(
    boundary_start,
    volume_start,
    diag_part,
    incident,
    kernel,
    elem_mats,
    trace_owner,
    trace_slot,
    return_owner,
    return_slot,
    face_match,
):
    devices = lax.axis_size(("row", "col"))
    row_devices = lax.axis_size("row")
    col_devices = lax.axis_size("col")
    device_self = lax.axis_index(("row", "col"))
    row_index = lax.axis_index("row")
    col_index = lax.axis_index("col")
    total_rows = trace_slot.shape[0]
    share_rows = total_rows // devices
    capacity = max(2, 2 * share_rows // devices)
    per_panel = col_devices // row_devices
    elem_count, node_count, columns = volume_start.shape
    face_count = face_match.shape[1]
    row_panel = boundary_start.shape[0]
    positions = jnp.arange(share_rows, dtype=jnp.int32)
    trace_blocks = trace_owner[:, 0].reshape(devices, share_rows)
    trace_slots = trace_slot.reshape(devices, share_rows)
    return_blocks = return_owner[:, 0].reshape(devices, share_rows)
    return_slots = return_slot.reshape(devices, share_rows)

    trace_send, _ = block_plan(trace_blocks, trace_slots, device_self, capacity)
    own_trace = lax.dynamic_slice_in_dim(trace_blocks, row_index * col_devices, col_devices, 0)
    own_places = jnp.broadcast_to(positions[None, :], (col_devices, share_rows))
    trace_take, trace_take_ok = jax.vmap(
        lambda r: block_plan(own_trace, own_places, r * col_devices + col_index, capacity)
    )(jnp.arange(row_devices, dtype=jnp.int32))
    trace_take = jnp.where(trace_take_ok, trace_take, -1).transpose(1, 0, 2)
    trace_take = trace_take.reshape(col_devices, 1, row_devices * capacity)
    own_return = lax.dynamic_slice_in_dim(return_blocks, col_index * row_devices, row_devices, 0)
    panel_places = jnp.arange(row_devices, dtype=jnp.int32)[:, None] * share_rows + positions[None, :]
    flux_send = jax.vmap(
        lambda d: block_plan(own_return, panel_places, row_index * col_devices + d, capacity)[0]
    )(jnp.arange(col_devices, dtype=jnp.int32))
    flux_take, flux_take_ok = block_plan(return_blocks, return_slots, device_self, capacity)
    slots = devices * capacity
    trace_send, flux_send = trace_send.reshape(slots), flux_send.reshape(slots)
    flux_take = jnp.where(flux_take_ok, flux_take, -1).reshape(1, slots)
    face_rows = face_match[:, :, None]

    share = lax.dynamic_slice_in_dim(boundary_start, col_index * share_rows, share_rows, 0)
    share, panel = exchange(False, False, share)
    volume_field = volume_start
    for sweep_index in range(ITERS):
        panel = panel.reshape(row_devices * share_rows, columns)

        volume_flat = volume_field.reshape(elem_count * node_count, columns)
        outgoing = jnp.take(volume_flat, trace_send, axis=0, mode="clip")
        arrived = lax.all_to_all(outgoing, "row", split_axis=0, concat_axis=0, tiled=True)
        arrived = arrived.reshape(row_devices, col_devices, capacity, columns).transpose(1, 0, 2, 3)
        trace_wide = halves(arrived.reshape(col_devices, row_devices * capacity, columns), 2)
        leaving = jnp.take(panel, flux_send, axis=0, mode="clip")
        landed = lax.all_to_all(leaving, "col", split_axis=0, concat_axis=0, tiled=True)
        lower_faces = passed_along(volume_field[:, node_count - face_count :, :], ("row", "col"), 1)
        middle = share - boundary_step * (diag_part[:, None] * share - incident)
        operands = (
            halves(panel, 1), trace_wide, trace_take, kernel, elem_mats, volume_field,
            halves(landed, 1), flux_take, halves(lower_faces, 2), face_rows, middle,
        )
        if sweep_index < ITERS - 1:
            volume_field, share, panel = exchange(True, False, *operands)
        else:
            volume_field, boundary_final = exchange(True, True, *operands)
    return (boundary_final.reshape(row_panel, columns), volume_field)


def solution(mesh):
    placed = (
        P("row", None),
        P(("row", "col"), None, None),
        P(("row", "col")),
        P(("row", "col"), None),
        P("row", "col"),
        P(("row", "col"), None, None),
        P(),
        P(),
        P(),
        P(),
        P(("row", "col"), None),
    )
    return jax.shard_map(
        shards,
        mesh=mesh,
        in_specs=placed,
        out_specs=(P("row", None), P(("row", "col"), None, None)),
        check_vma=False,
    )
```

```python
import functools

import jax
import jax.numpy as jnp
from jax import lax
from jax.experimental import pallas as pl
from jax.experimental.pallas import tpu as pltpu
from jax.sharding import PartitionSpec as P

ITERS = 3


boundary_step = 0.5
volume_step = 0.6
face_weight = 0.5


def passed_along(block, axis, distance):
    devices = range(lax.axis_size(axis))
    route = [(i - distance, i) for i in devices if i - distance in devices]
    return lax.ppermute(block, axis, route)


def exchange_kernel(reduces, finishes, *refs):
    rows_n, cols_n = lax.axis_size("row"), lax.axis_size("col")
    pairs = cols_n // 2
    per_panel = cols_n // rows_n
    r, c = lax.axis_index("row"), lax.axis_index("col")
    z, h = c // 2, c % 2
    partner = z * 2 + (1 - h)
    target_row, target_col = c % rows_n, r * per_panel + c // rows_n
    source_row, source_col = c // per_panel, (c % per_panel) * rows_n + r
    stays = (target_row == r) & (target_col == c)

    if reduces:
        panel_wide, trace_wide, trace_take, kernel, elem_mats, volume = refs[:6]
        flux_send, flux_take, face_wide, face_match, middle, volume_out = refs[6:12]
        refs = refs[12:]
    else:
        middle, refs = refs[0], refs[1:]
    if finishes:
        out, refs = refs[0], refs[1:]
    else:
        share, out, refs = refs[0], refs[1], refs[2:]
    if reduces:
        from_pair, summed_pair, from_line, refs = refs[0], refs[1], refs[2], refs[3:]
        pair_send, pair_recv, line_send, line_recv, refs = refs[0], refs[1], refs[2], refs[3], refs[4:]
        partial, kernel_blocks, elem_blocks, kernel_sem, elem_sem = refs[:5]
        leaving, landed, flux_wide, flux_out, flux_in = refs[5:10]
        refs = refs[10:]
    if finishes:
        out_send, out_recv, back_send, back_recv = refs
    else:
        move_send, move_recv, row_send, row_recv = refs

    barrier = pltpu.get_barrier_semaphore()

    def greet(row, col):
        pl.semaphore_signal(barrier, inc=1, device_id=(row, col), device_id_type=pl.DeviceIdType.MESH)

    greeted = 0
    if reduces:
        for step in range(1, cols_n):
            greet(r, (c + step) % cols_n)
        greeted += cols_n - 1
    if not finishes:
        for step in range(1, rows_n):
            greet((r + step) % rows_n, c)
        greeted += rows_n - 1

        @pl.when(jnp.logical_not(stays))
        def _():
            greet(source_row, source_col)

        greeted += jnp.where(stays, 0, 1)

    pl.semaphore_wait(barrier, greeted)

    def remote(src, dst, send, recv, row, col):
        return pltpu.make_async_remote_copy(
            src_ref=src,
            dst_ref=dst,
            send_sem=send,
            recv_sem=recv,
            device_id=(row, col),
            device_id_type=pl.DeviceIdType.MESH,
        )

    if reduces:
        share_rows, columns = middle.shape
        tile = min(128, share_rows)
        elem_count, node_count, _ = volume.shape
        face_count = face_match.shape[1]

        def parts(block):
            high = block.astype(jnp.bfloat16)
            low = (block - high.astype(jnp.float32)).astype(jnp.bfloat16)
            return high, low

        def product(left, right):
            return jnp.dot(left, right, preferred_element_type=jnp.float32)

        def one_hot(hits):
            return jnp.where(hits, 1.0, 0.0).astype(jnp.bfloat16)

        def product_block(block, slot):
            def step(t, carry):
                rows = pl.ds(pl.multiple_of(t * tile, tile), tile)
                high, low = parts(kernel_blocks[slot, rows, :])
                place = lax.broadcasted_iota(jnp.int32, (tile, trace_wide.shape[1]), 0) + t * tile
                wide = product(high, panel_wide[...]) + product(low, panel_wide[...])
                wide -= product(one_hot(place == trace_take[block]), trace_wide[block])
                partial[block, rows, :] = wide[:, :columns] + wide[:, columns:]
                return carry

            lax.fori_loop(0, share_rows // tile, step, 0)

        def volume_step_of(e, carry):
            field = volume[e]
            high, low = parts(elem_blocks[e])
            field_wide = jnp.concatenate(parts(field), axis=1)
            wide = product(high, field_wide) + product(low, field_wide)
            place = lax.broadcasted_iota(jnp.int32, (node_count, flux_wide.shape[0]), 0) + e * node_count
            wide -= product(one_hot(place == flux_take[...]), flux_wide[...])
            volume_out[e] = field - volume_step * (field + wide[:, :columns] + wide[:, columns:])
            node = lax.broadcasted_iota(jnp.int32, (face_count, face_count), 1)
            face = product(one_hot(node == face_match[e]), face_wide[e])
            matched = face[:, :columns] + face[:, columns:]
            volume_out[e, :face_count, :] += volume_step * face_weight * matched
            return carry

        elem_load = pltpu.make_async_copy(elem_mats, elem_blocks, elem_sem)
        order = []
        for step in range(1, pairs + 1):
            other = (z + step) % pairs
            order += [other * 2 + (1 - h), other * 2 + h]

        def load(i):
            return pltpu.make_async_copy(
                kernel.at[pl.ds(pl.multiple_of(order[i] * share_rows, share_rows), share_rows), :],
                kernel_blocks.at[i % 2],
                kernel_sem.at[i % 2],
            )

        load(0).start()
        elem_load.start()

        def picked(member):
            node = lax.broadcasted_iota(jnp.int32, (flux_send.shape[1], panel_wide.shape[0]), 1)
            wide = product(one_hot(node == flux_send[member]), panel_wide[...])
            return wide[:, :columns] + wide[:, columns:]

        flux_copies = []
        for step in range(1, cols_n):
            member = (c + step) % cols_n
            leaving[step - 1] = picked(member)
            copy = remote(
                leaving.at[step - 1], landed.at[c], flux_out.at[step - 1], flux_in.at[step - 1], r, member
            )
            copy.start()
            flux_copies.append(copy)
        landed[c] = picked(c)
        pair_copies = []
        line_copies = []

        def pass_on(step):
            other = (z + step) % pairs
            pair_copies[step - 1].wait_recv()
            summed_pair[step - 1] = from_pair[step - 1] + partial[other * 2 + h]
            copy = remote(
                summed_pair.at[step - 1], from_line.at[step - 1],
                line_send.at[step - 1], line_recv.at[step - 1], r, other * 2 + h,
            )
            copy.start()
            line_copies.append(copy)

        for i in range(2 * pairs):
            if i + 1 < 2 * pairs:
                load(i + 1).start()
            load(i).wait()
            product_block(order[i], i % 2)
            if i % 2 == 0:
                copy = remote(
                    partial.at[order[i]], from_pair.at[i // 2],
                    pair_send.at[i // 2], pair_recv.at[i // 2], r, partner,
                )
                copy.start()
                pair_copies.append(copy)
            elif i // 2 + 1 < pairs:
                pass_on(i // 2 + 1)
        elem_load.wait()
        for copy in flux_copies:
            copy.wait_recv()
        flux_wide[...] = jnp.concatenate(parts(landed[...].reshape(flux_wide.shape[0], columns)), axis=1)
        lax.fori_loop(0, elem_count // 2, volume_step_of, 0)
        pair_copies[pairs - 1].wait_recv()
        total = from_pair[pairs - 1] + partial[z * 2 + h]
        summed_pair[pairs - 1] = total
        for step in range(1, pairs):
            line_copies[step - 1].wait_recv()
            summed_pair[pairs - 1] += from_line[step - 1]
        fresh = middle[...] - boundary_step * summed_pair[pairs - 1]
        if finishes:
            out[c] = fresh
        else:
            share[...] = fresh
    else:
        share[...] = middle[...]

    if finishes:
        sent = []
        for step in range(1, pairs):
            copy = remote(
                out.at[c], out.at[c], out_send.at[step - 1], out_recv.at[step - 1],
                r, ((z + step) % pairs) * 2 + h,
            )
            copy.start()
            sent.append(copy)
        back = [remote(out.at[c], out.at[c], back_send.at[0], back_recv.at[0], r, partner)]
        back[0].start()
        for step in range(1, pairs):
            origin = ((z - step + pairs) % pairs) * 2 + h
            sent[step - 1].wait_recv()
            copy = remote(
                out.at[origin], out.at[origin], back_send.at[step], back_recv.at[step], r, partner
            )
            copy.start()
            back.append(copy)
        if reduces:
            lax.fori_loop(elem_count // 2, elem_count, volume_step_of, 0)
        for copy in back:
            copy.wait_recv()
        for copy in sent + back:
            copy.wait_send()
    else:
        @pl.when(stays)
        def _():
            out[r] = share[...]

        move = remote(share, out.at[target_row], move_send, move_recv, target_row, target_col)

        @pl.when(jnp.logical_not(stays))
        def _():
            move.start()
            move.wait_recv()

        sent = []
        for step in range(1, rows_n):
            copy = remote(
                out.at[r], out.at[r], row_send.at[step - 1], row_recv.at[step - 1],
                (r + step) % rows_n, c,
            )
            copy.start()
            sent.append(copy)
        if reduces:
            lax.fori_loop(elem_count // 2, elem_count, volume_step_of, 0)
        for copy in sent:
            copy.wait_recv()
        for copy in sent:
            copy.wait_send()

        @pl.when(jnp.logical_not(stays))
        def _():
            move.wait_send()

    if reduces:
        for copy in pair_copies + line_copies + flux_copies:
            copy.wait_send()


def exchange(reduces, finishes, *operands):
    rows_n, cols_n = lax.axis_size("row"), lax.axis_size("col")
    pairs = cols_n // 2
    rows, columns = operands[-1].shape
    block = (rows, columns)
    in_vmem = pl.BlockSpec(memory_space=pltpu.VMEM)
    if finishes:
        shapes = [jax.ShapeDtypeStruct((cols_n,) + block, jnp.float32)]
    else:
        shapes = [
            jax.ShapeDtypeStruct(block, jnp.float32),
            jax.ShapeDtypeStruct((rows_n,) + block, jnp.float32),
        ]
    scratch = []
    in_specs = [in_vmem] * len(operands)
    if reduces:
        kernel, elem_mats, volume = operands[3:6]
        shapes = [jax.ShapeDtypeStruct(volume.shape, jnp.float32)] + shapes
        in_specs[3] = in_specs[4] = pl.BlockSpec(memory_space=pl.ANY)
        scratch += [pltpu.VMEM((pairs,) + block, jnp.float32), pltpu.VMEM((pairs,) + block, jnp.float32)]
        scratch += [pltpu.VMEM((pairs - 1,) + block, jnp.float32)]
        scratch += [pltpu.SemaphoreType.DMA((pairs,))] * 2 + [pltpu.SemaphoreType.DMA((pairs - 1,))] * 2
        scratch += [
            pltpu.VMEM((cols_n,) + block, jnp.float32),
            pltpu.VMEM((2, rows, kernel.shape[1]), jnp.float32),
            pltpu.VMEM(elem_mats.shape, jnp.float32),
            pltpu.SemaphoreType.DMA((2,)),
            pltpu.SemaphoreType.DMA,
        ]
        slots = operands[6].shape[1]
        scratch += [
            pltpu.VMEM((cols_n - 1, slots, columns), jnp.float32),
            pltpu.VMEM((cols_n, slots, columns), jnp.float32),
            pltpu.VMEM((cols_n * slots, 2 * columns), jnp.bfloat16),
        ]
        scratch += [pltpu.SemaphoreType.DMA((cols_n - 1,))] * 2
    if finishes:
        scratch += [pltpu.SemaphoreType.DMA((pairs - 1,))] * 2 + [pltpu.SemaphoreType.DMA((pairs,))] * 2
    else:
        scratch += [pltpu.SemaphoreType.DMA] * 2 + [pltpu.SemaphoreType.DMA((rows_n - 1,))] * 2
    return pl.pallas_call(
        functools.partial(exchange_kernel, reduces, finishes),
        out_shape=shapes,
        in_specs=in_specs,
        out_specs=[in_vmem] * len(shapes),
        scratch_shapes=scratch,
        compiler_params=pltpu.CompilerParams(
            collective_id=int(reduces) + int(finishes), has_side_effects=True, vmem_limit_bytes=(48 << 20) if reduces else (8 << 20)
        ),
        cost_estimate=pl.CostEstimate(flops=1000, bytes_accessed=150_000_000, transcendentals=0),
    )(*operands)


def halves(block, axis):
    high = lax.reduce_precision(block, 8, 7)
    low = block - high
    return jnp.concatenate([high.astype(jnp.bfloat16), low.astype(jnp.bfloat16)], axis=axis)


def block_plan(owner_blocks, slot_blocks, device_self, capacity):
    mine_rows = owner_blocks == device_self
    rank_rows = jnp.cumsum(mine_rows.astype(jnp.int32), axis=1) - 1
    places = jnp.arange(capacity, dtype=jnp.int32)
    select = mine_rows[:, None, :] & (rank_rows[:, None, :] == places[None, :, None])
    index = jnp.sum(jnp.where(select, slot_blocks[:, None, :], 0), axis=2)
    valid_slot = jnp.any(select, axis=2)
    return (index, valid_slot)


def shards(
    boundary_start,
    volume_start,
    diag_part,
    incident,
    kernel,
    elem_mats,
    trace_owner,
    trace_slot,
    return_owner,
    return_slot,
    face_match,
):
    devices = lax.axis_size(("row", "col"))
    row_devices = lax.axis_size("row")
    col_devices = lax.axis_size("col")
    device_self = lax.axis_index(("row", "col"))
    row_index = lax.axis_index("row")
    col_index = lax.axis_index("col")
    total_rows = trace_slot.shape[0]
    share_rows = total_rows // devices
    capacity = max(2, 2 * share_rows // devices)
    per_panel = col_devices // row_devices
    elem_count, node_count, columns = volume_start.shape
    face_count = face_match.shape[1]
    row_panel = boundary_start.shape[0]
    positions = jnp.arange(share_rows, dtype=jnp.int32)
    trace_blocks = trace_owner[:, 0].reshape(devices, share_rows)
    trace_slots = trace_slot.reshape(devices, share_rows)
    return_blocks = return_owner[:, 0].reshape(devices, share_rows)
    return_slots = return_slot.reshape(devices, share_rows)

    trace_send, _ = block_plan(trace_blocks, trace_slots, device_self, capacity)
    own_trace = lax.dynamic_slice_in_dim(trace_blocks, row_index * col_devices, col_devices, 0)
    own_places = jnp.broadcast_to(positions[None, :], (col_devices, share_rows))
    trace_take, trace_take_ok = jax.vmap(
        lambda r: block_plan(own_trace, own_places, r * col_devices + col_index, capacity)
    )(jnp.arange(row_devices, dtype=jnp.int32))
    trace_take = jnp.where(trace_take_ok, trace_take, -1).transpose(1, 0, 2)
    trace_take = trace_take.reshape(col_devices, 1, row_devices * capacity)
    own_return = lax.dynamic_slice_in_dim(return_blocks, col_index * row_devices, row_devices, 0)
    panel_places = jnp.arange(row_devices, dtype=jnp.int32)[:, None] * share_rows + positions[None, :]
    flux_send = jax.vmap(
        lambda d: block_plan(own_return, panel_places, row_index * col_devices + d, capacity)[0]
    )(jnp.arange(col_devices, dtype=jnp.int32))
    flux_take, flux_take_ok = block_plan(return_blocks, return_slots, device_self, capacity)
    slots = devices * capacity
    trace_send = trace_send.reshape(slots)
    flux_send = flux_send.reshape(col_devices, row_devices * capacity, 1)
    flux_take = jnp.where(flux_take_ok, flux_take, -1).reshape(1, slots)
    face_rows = face_match[:, :, None]

    share = lax.dynamic_slice_in_dim(boundary_start, col_index * share_rows, share_rows, 0)
    share, panel = exchange(False, False, share)
    volume_field = volume_start
    for sweep_index in range(ITERS):
        panel = panel.reshape(row_devices * share_rows, columns)

        volume_flat = volume_field.reshape(elem_count * node_count, columns)
        outgoing = jnp.take(volume_flat, trace_send, axis=0, mode="clip")
        arrived = lax.all_to_all(outgoing, "row", split_axis=0, concat_axis=0, tiled=True)
        arrived = arrived.reshape(row_devices, col_devices, capacity, columns).transpose(1, 0, 2, 3)
        trace_wide = halves(arrived.reshape(col_devices, row_devices * capacity, columns), 2)
        lower_faces = passed_along(volume_field[:, node_count - face_count :, :], ("row", "col"), 1)
        middle = share - boundary_step * (diag_part[:, None] * share - incident)
        operands = (
            halves(panel, 1), trace_wide, trace_take, kernel, elem_mats, volume_field,
            flux_send, flux_take, halves(lower_faces, 2), face_rows, middle,
        )
        if sweep_index < ITERS - 1:
            volume_field, share, panel = exchange(True, False, *operands)
        else:
            volume_field, boundary_final = exchange(True, True, *operands)
    return (boundary_final.reshape(row_panel, columns), volume_field)


def solution(mesh):
    placed = (
        P("row", None),
        P(("row", "col"), None, None),
        P(("row", "col")),
        P(("row", "col"), None),
        P("row", "col"),
        P(("row", "col"), None, None),
        P(),
        P(),
        P(),
        P(),
        P(("row", "col"), None),
    )
    return jax.shard_map(
        shards,
        mesh=mesh,
        in_specs=placed,
        out_specs=(P("row", None), P(("row", "col"), None, None)),
        check_vma=False,
    )
```
